32 devices in a mesh: row: 4 (over y, x), col: 8 (over z, core).
Axes of the slice: x: 2, y: 2, z: 4, core: 2. Of those that a mesh axis runs over, the one named last changes fastest.
Arguments:
- momentum: float32 [4608, 8192], P('row', 'col'), may hold values from -37 to 37
Outputs:
- update: float32 [4608, 8192], P('row', 'col')
The draws below stay inside these ranges and needn't reach their ends.
All inputs are finite; a program needn't handle non-finite values.
Results may differ from the reference program's by a relative error of at most 0.0049.
Values may be sent and summed in bfloat16 or wider, within the bound.
No kernel may reach another device: no remote copies, remote signals or barrier semaphores. Data moves between devices by JAX's collectives and lax.ppermute only.
A program may use at most 128 MiB of HBM per device.

```python
import math
import jax
import jax.numpy as jnp

ROWS = 4608
COLS = 8192


def draw_momentum(key, part):
    keys = jax.random.split(key, 3)
    row_pos = jnp.arange(ROWS, dtype=jnp.float32) / ROWS
    col_pos = jnp.arange(COLS, dtype=jnp.float32) / COLS
    ramp_rate = 0.5 * math.log(3.0)
    row_scale = jnp.exp(ramp_rate * row_pos + 0.35 * jax.random.uniform(keys[1], (ROWS,), jnp.float32))
    col_scale = jnp.exp(ramp_rate * col_pos + 0.35 * jax.random.uniform(keys[2], (COLS,), jnp.float32))
    base = jnp.clip(jax.random.normal(keys[0], (ROWS, COLS), jnp.float32), -6.0, 6.0)
    return base * row_scale[:, None] * col_scale[None, :]


def setup_inputs(seed: int = 0) -> dict:
    seeds = jax.random.split(jax.random.key(seed), 2)
    momentum = draw_momentum(jax.random.fold_in(seeds[1], 71), 0)
    return {"momentum": momentum}


quintic_a = 3.4445
quintic_b = -4.775
quintic_c = 2.0315

def reference(momentum):
    norm_squares = jnp.sum(momentum * momentum)
    factor = 0.6 * math.sqrt(ROWS) / (jnp.sqrt(norm_squares) + 1e-07)
    scaled = (momentum * factor).astype(jnp.bfloat16)
    gram = jnp.dot(scaled, scaled.T, preferred_element_type=jnp.float32).astype(jnp.bfloat16)
    squared = jnp.dot(gram, gram, preferred_element_type=jnp.float32)
    poly = (quintic_b * gram.astype(jnp.float32) + quintic_c * squared).astype(jnp.bfloat16)
    product = jnp.dot(poly, scaled, preferred_element_type=jnp.float32)
    return math.sqrt(COLS) * (quintic_a * scaled.astype(jnp.float32) + product)
```

```python
import math

import jax
import jax.numpy as jnp
from jax import lax
from jax.sharding import PartitionSpec as P

quintic_a = 3.4445
quintic_b = -4.775
quintic_c = 2.0315

CORES = 2
ROW_CHUNKS = 4

bf16 = jnp.bfloat16
f32 = jnp.float32


def rows_product(left, right):
    return lax.dot_general(
        left, right, (((1,), (1,)), ((), ())), preferred_element_type=f32
    )


def product(left, right):
    return jnp.dot(left, right, preferred_element_type=f32)


def ring(size, step):
    order = [i ^ (i >> 1) for i in range(size)]
    if sorted(order) != list(range(size)):
        order = list(range(size))
    return [(order[i], order[(i + step) % size]) for i in range(size)]


def sum_of_all(value):
    for axis in ("row", "col"):
        size = lax.axis_size(axis)
        received = [
            lax.ppermute(value, axis, [(i, (i + d) % size) for i in range(size)])
            for d in range(1, size)
        ]
        for other in received:
            value = value + other
    return value


def ring_gather(chunks):
    size = lax.axis_size("row")
    forth, back = ring(size, 1), ring(size, -1)
    blocks, ahead, behind = [chunks], chunks, chunks
    for _ in range((size - 1) // 2):
        ahead, behind = zip(
            *[
                (lax.ppermute(a, "row", forth), lax.ppermute(b, "row", back))
                for a, b in zip(ahead, behind)
            ]
        )
        blocks += [list(ahead), list(behind)]
    if size % 2 == 0:
        half = len(chunks) // 2
        blocks.append(
            [lax.ppermute(a, "row", forth) for a in ahead[:half]]
            + [lax.ppermute(b, "row", back) for b in behind[half:]]
        )
    return blocks


def swap_cores(value):
    size = lax.axis_size("col")
    return lax.ppermute(value, "col", [(c, c ^ 1) for c in range(size)])


def line_sum(part):
    chips = lax.axis_size("col") // CORES
    chip = lax.axis_index("col") // CORES
    half = chips // 2

    def send(value, moves):
        pairs = [
            (a * CORES + k, b * CORES + k) for a, b in moves for k in range(CORES)
        ]
        return lax.ppermute(value, "col", pairs)

    for i in range(half - 1):
        moves = [(i, i + 1), (chips - 1 - i, chips - 2 - i)]
        part = part + send(part.astype(bf16), moves).astype(f32)
    moves = [(half - 1, half), (half, half - 1)]
    total = (part + send(part.astype(bf16), moves).astype(f32)).astype(bf16)
    for i in reversed(range(half - 1)):
        moves = [(i + 1, i), (chips - 2 - i, chips - 1 - i)]
        received = send(total, moves)
        total = jnp.where((chip == i) | (chip == chips - 1 - i), received, total)
    return total


def body(momentum):
    m, n = momentum.shape
    all_rows = m * lax.axis_size("row")
    all_cols = n * lax.axis_size("col")
    core = lax.axis_index("col") % CORES

    squares = jnp.full((8, 128), jnp.sum(momentum * momentum))
    norm_squares = sum_of_all(squares)[0, 0]
    factor = 0.6 * math.sqrt(all_rows) / (jnp.sqrt(norm_squares) + 1e-07)
    scaled = (momentum * factor).astype(bf16)

    chunks = [scaled[: m // 2], scaled[m // 2 :]]
    blocks = [jnp.concatenate(b, 0) for b in ring_gather(chunks)]

    by_core = scaled.reshape(ROW_CHUNKS, CORES, -1, n)
    mine = lax.dynamic_index_in_dim(by_core, core, 1, keepdims=False)
    other = lax.dynamic_index_in_dim(by_core, 1 - core, 1, keepdims=False)

    def gram_rows(first, last, block):
        k = last - first
        theirs = rows_product(other[first:last].reshape(-1, n), block).astype(bf16)
        received = swap_cores(theirs).astype(f32)
        part = rows_product(mine[first:last].reshape(-1, n), block) + received
        total = line_sum(part)
        swapped = swap_cores(total)
        low = jnp.where(core == 0, total, swapped).reshape(k, 1, -1, m)
        high = jnp.where(core == 0, swapped, total).reshape(k, 1, -1, m)
        return jnp.concatenate([low, high], 1).reshape(-1, m)

    splits = [[(0, 4)]] + [[(0, 2), (2, 4)]] * (len(blocks) - 2) + [[(0, 1), (1, 2), (2, 4)]]
    gram = [[None] * len(s) for s in splits]
    for b in range(len(blocks)):
        for i, (first, last) in enumerate(splits[b]):
            gram[b][i] = gram_rows(first, last, blocks[b])
    gram = [jnp.concatenate(g, 0) for g in gram]

    rows = m // ROW_CHUNKS
    inner = []
    for j in range(ROW_CHUNKS):
        part = slice(j * rows, (j + 1) * rows)
        twice = sum(product(g[part], b) for g, b in zip(gram, blocks))
        inner.append(
            (quintic_b * scaled[part].astype(f32) + quintic_c * twice).astype(bf16)
        )
    inner_blocks = ring_gather(inner)
    total = sum(
        product(g, jnp.concatenate(u, 0)) for g, u in zip(gram, inner_blocks)
    )
    return math.sqrt(all_cols) * (quintic_a * scaled.astype(f32) + total)


def solution(mesh):
    placed = (P("row", "col"),)
    return jax.shard_map(
        body, mesh=mesh, in_specs=placed, out_specs=P("row", "col"), check_vma=False
    )
```
